128 devices in a mesh: patch: 16 (over z, x_lo, core), head: 8 (over y, x_hi).
Axes of the slice: x: 4 (x_hi: 2, x_lo: 2; x = x_hi * 2 + x_lo), y: 4, z: 4, core: 2. Of those that a mesh axis runs over, the one named last changes fastest.
Arguments:
- img_qkv: bfloat16 [8192, 9216], P(('patch', 'head')), may hold values from -8 to 8
- txt_qkv: bfloat16 [512, 9216], P('head'), may hold values from -8 to 8
- stale_kv: bfloat16 [2, 8192, 3072], P(None, 'patch', 'head'), may hold values from -8 to 8
- residual: bfloat16 [8192, 3072], P(('patch', 'head')), may hold values from -4 to 4
- gate_scale: float32 [3072], replicated, may hold values from 0.5 to 3
- proj_weight: bfloat16 [3072, 3072], replicated, may hold values from -0.109375 to 0.109375
Outputs:
- image_out: bfloat16 [8192, 3072], P(('patch', 'head'))
- text_attn: bfloat16 [512, 3072], P('head')
The draws below stay inside these ranges and needn't reach their ends.
All inputs are finite; a program needn't handle non-finite values.
Results may differ from the reference program's by a relative error of at most 0.0075.
Values may be sent and summed in bfloat16 or wider, within the bound.
A program may use at most 192 MiB of HBM per device.

```python
import math
import jax
import jax.numpy as jnp
from jax import lax

H = 24
HD = 128
TXT = 512
D = 3072
GROUP = 512
IMG = 8192
N_PATCH = 16


def draw_rows(key, rows):
    row_width = H * HD
    base = jax.random.fold_in(key, 11)
    entries = jnp.clip(1.6 * jax.random.normal(base, (rows, 3 * row_width), jnp.float32), -8.0, 8.0)
    return entries


def draw_img_qkv(key, part):
    return draw_rows(key, IMG).astype(jnp.bfloat16)


def draw_txt_qkv(key, part):
    return draw_rows(key, TXT).astype(jnp.bfloat16)


def steps_of(own_key, shape, split, low, top_value):
    def one(axis_at, blocks):
        heights = jax.random.uniform(jax.random.fold_in(jax.random.fold_in(own_key, 6), axis_at), (blocks,), jnp.float32, low / len(split), top_value / len(split))
        return jnp.repeat(jnp.exp(heights), shape[axis_at] // blocks).reshape((-1,) + (1,) * (len(shape) - axis_at - 1))

    factor_of = one(*split[0])
    for cut in split[1:]:
        factor_of = factor_of * one(*cut)
    return factor_of


def gaussian(own_key, extent, spread, most, split=(), kind=jnp.bfloat16):
    gain = steps_of(own_key, extent, split, -0.22, 0.18) if split else 1.0
    values = jax.random.normal(own_key, extent, jnp.float32) * spread * gain
    return jnp.minimum(jnp.maximum(values, -most), most).astype(kind)


def setup_inputs(seed: int = 0) -> dict:
    splits = jax.random.split(jax.random.key(seed), 7)
    img_qkv = draw_img_qkv(jax.random.fold_in(splits[6], 71), 0)
    txt_qkv = draw_txt_qkv(jax.random.fold_in(splits[6], 71), 0)
    stale_kv = gaussian(splits[2], (2, IMG, D), 1.6, 8.0, ((1, 16), (2, 8)))
    residual = gaussian(splits[3], (IMG, D), 0.5, 4.0, ((0, 128),))
    gate_scale = jnp.clip(jnp.exp(jax.random.uniform(splits[4], (D,), jnp.float32, math.log(0.5), math.log(3.0))), 0.5, 3.0)
    proj_weight = gaussian(splits[5], (D, D), D ** -0.5, 0.109375)
    return {"img_qkv": img_qkv, "txt_qkv": txt_qkv, "stale_kv": stale_kv, "residual": residual, "gate_scale": gate_scale, "proj_weight": proj_weight}


def attend_head(queries, key_rows, values):
    scores = jnp.dot(queries, key_rows.T, preferred_element_type=jnp.float32) * (1.0 / math.sqrt(HD))
    row_max = lax.optimization_barrier(jnp.max(scores, axis=1, keepdims=True))
    shifted = jnp.exp(scores - row_max)
    row_sum = lax.optimization_barrier(jnp.sum(shifted, axis=1, keepdims=True))
    weights = shifted.astype(jnp.bfloat16)
    mixed_rows = jnp.dot(weights, values, preferred_element_type=jnp.float32)
    return (mixed_rows / row_sum).astype(jnp.bfloat16)

def attend_heads(queries, key_rows, values):
    moved = (jnp.moveaxis(queries, 1, 0), jnp.moveaxis(key_rows, 1, 0), jnp.moveaxis(values, 1, 0))
    result = lax.map(lambda triple: attend_head(triple[0], triple[1], triple[2]), moved)
    return jnp.moveaxis(result, 0, 1)

def reference(img_qkv, txt_qkv, stale_kv, residual, gate_scale, proj_weight):
    img_parts = img_qkv.reshape(IMG, 3, H, HD)
    txt_parts = txt_qkv.reshape(TXT, 3, H, HD)
    stale_keys = stale_kv[0].reshape(IMG, H, HD)
    stale_values = stale_kv[1].reshape(IMG, H, HD)
    text_keys = txt_parts[:, 1]
    text_values = txt_parts[:, 2]

    def one_group(group_index):
        first_row = (group_index * GROUP).astype(jnp.int32)
        fresh_keys = lax.dynamic_slice_in_dim(img_parts[:, 1], first_row, GROUP, 0)
        fresh_values = lax.dynamic_slice_in_dim(img_parts[:, 2], first_row, GROUP, 0)
        group_keys = lax.dynamic_update_slice_in_dim(stale_keys, fresh_keys, first_row, 0)
        group_values = lax.dynamic_update_slice_in_dim(stale_values, fresh_values, first_row, 0)
        queries = lax.dynamic_slice_in_dim(img_parts[:, 0], first_row, GROUP, 0)
        return attend_heads(queries, jnp.concatenate([text_keys, group_keys], axis=0), jnp.concatenate([text_values, group_values], axis=0))
    image_attn = lax.map(one_group, jnp.arange(N_PATCH, dtype=jnp.int32)).reshape(IMG, D)
    text_attn = attend_heads(txt_parts[:, 0], jnp.concatenate([text_keys, stale_keys], axis=0), jnp.concatenate([text_values, stale_values], axis=0)).reshape(TXT, D)
    projected = jnp.dot(image_attn, proj_weight, preferred_element_type=jnp.float32)
    image_out = (residual.astype(jnp.float32) + gate_scale * projected).astype(jnp.bfloat16)
    return (image_out, text_attn)
```

```python
import math

import jax
import jax.numpy as jnp
from jax import lax
from jax.experimental import pallas as pl
from jax.experimental.pallas import tpu as pltpu
from jax.sharding import PartitionSpec as P

HD = 128
NH = 3
W3 = NH * HD
D = 3072
N_HEAD = 8
GR = 512
MINE = GR + 32
ROWS = 2 * MINE
LOG2E_SCALE = math.log2(math.e) / math.sqrt(HD)
MESH = pl.DeviceIdType.MESH
SLOTS = (1, 2, 6, 3, 7, 4, 5)


def pick(i, values):
    out = jnp.int32(values[-1])
    for n, value in enumerate(values[:-1]):
        out = jnp.where(i == n, jnp.int32(value), out)
    return out


def kernel(
    img, txt, stale, residual, gate, weight,
    out_img, out_txt,
    q_buf, tq, kv, fresh, tkv, acc, mx, wbuf, po, pr, ls, lr, fin, tfin, tattn, attn, total, res, gat, obuf,
    s_q, r_q, s_p, r_p, s_t, r_t, s_f, r_f, s_x, r_x, s_k, r_k, s_o, r_o, s_b, r_b, s_ta, r_ta, s_tb, r_tb, lsem, wsem,
):
    p = lax.axis_index("patch")
    h = lax.axis_index("head")
    z = p // 4
    x = (p // 2) % 2
    c = p % 2
    t = z * 2 + c
    sib = p + 1 - 2 * c
    part = p + 2 - 4 * x
    up = ((z + 1) % 4) * 4 + x * 2 + c
    down = ((z + 3) % 4) * 4 + x * 2 + c
    text_here = (h // 4) == x

    def rcopy(src, dst, ssem, rsem, to):
        return pltpu.make_async_remote_copy(
            src_ref=src, dst_ref=dst, send_sem=ssem, recv_sem=rsem, device_id=to, device_id_type=MESH
        )

    def peer(i):
        return (h + i) % N_HEAD

    def cols(base, head):
        return pl.ds(pl.multiple_of(base + head * W3, 128), W3)

    loads = [
        pltpu.make_async_copy(img.at[:, cols(0, h)], q_buf.at[pl.ds(pl.multiple_of(64 * h, 64), 64), :], lsem.at[0]),
        pltpu.make_async_copy(txt.at[pl.ds(pl.multiple_of(8 * t, 8), 8), cols(0, h)], tq.at[h], lsem.at[1]),
        pltpu.make_async_copy(stale, kv.at[0], lsem.at[2]),
        pltpu.make_async_copy(img.at[:, cols(D, h)], fresh.at[0, pl.ds(pl.multiple_of(64 * h, 64), 64), :], lsem.at[3]),
        pltpu.make_async_copy(img.at[:, cols(2 * D, h)], fresh.at[1, pl.ds(pl.multiple_of(64 * h, 64), 64), :], lsem.at[4]),
        pltpu.make_async_copy(residual, res, lsem.at[5]),
        pltpu.make_async_copy(gate, gat, lsem.at[6]),
    ]
    for one in loads:
        one.start()
    wloads = []
    for j in range(NH):
        for g in range(N_HEAD):
            one = pltpu.make_async_copy(
                weight.at[pl.ds((NH * g + j) * HD, HD), :], wbuf.at[j, pl.ds(g * HD, HD), :], wsem.at[j * N_HEAD + g]
            )
            wloads.append(one)
    text_rows = pl.ds(pl.multiple_of(64 * (h % 4), 64), 64)
    tlocal = [
        pltpu.make_async_copy(txt.at[:, cols(D * (1 + n), h)], tkv.at[n, text_rows, :], lsem.at[7 + n]) for n in range(2)
    ]

    @pl.when(text_here)
    def _():
        for one in tlocal:
            one.start()

    barrier = pltpu.get_barrier_semaphore()
    greeted = 0
    for i in range(1, N_HEAD):
        pl.semaphore_signal(barrier, inc=1, device_id=(p, peer(i)), device_id_type=MESH)
        greeted += 1
    for i in range(N_HEAD):
        pl.semaphore_signal(barrier, inc=1, device_id=(part, peer(i)), device_id_type=MESH)
        greeted += 1
    for i in range(1, 16):
        other = (p + i) % 16

        @pl.when(other != part)
        def _():
            pl.semaphore_signal(barrier, inc=1, device_id=(other, h), device_id_type=MESH)

    greeted += 14
    pl.semaphore_wait(barrier, greeted)

    own_rows = pl.ds(pl.multiple_of(64 * h, 64), 64)
    part_rows = pl.ds(pl.multiple_of(MINE + 64 * h, 32), 64)
    sends = []

    def q_copy(i):
        to = peer(i)
        return rcopy(img.at[:, cols(0, to)], q_buf.at[own_rows, :], s_q.at[i], r_q.at[h], (p, to))

    def p_copy(i):
        to = peer(i)
        return rcopy(img.at[:, cols(0, to)], q_buf.at[part_rows, :], s_p.at[i], r_p.at[h], (part, to))

    def t_copy(i):
        to = peer(i)
        return rcopy(
            txt.at[pl.ds(pl.multiple_of(8 * t, 8), 8), cols(0, to)], tq.at[h], s_t.at[i], r_t.at[h], (p, to)
        )

    def f_copy(i, n):
        to = peer(i)
        return rcopy(
            img.at[:, cols(D * (1 + n), to)], fresh.at[n, own_rows, :], s_f.at[n, i], r_f.at[n, h], (p, to)
        )

    def x_copy(i, n):
        to = peer(i)
        return rcopy(
            txt.at[:, cols(D * (1 + n), to)], tkv.at[n, text_rows, :], s_x.at[n, i], r_x.at[n, h % 4], (p, to)
        )

    def hs(j):
        return pl.ds(j * HD, HD)

    def k_copy(j, n):
        to, slot = ((sib, 1), (up, 2), (down, 6))[n]
        return rcopy(
            stale.at[:, :, hs(j)], kv.at[slot, :, :, hs(j)], s_k.at[j, n], r_k.at[j, slot], (to, h)
        )

    def z_forward(j):
        src = 2 + 4 * c
        to = ((z + 1 + 2 * c) % 4) * 4 + x * 2 + c
        return rcopy(kv.at[src, :, :, hs(j)], kv.at[4, :, :, hs(j)], s_k.at[j, 3], r_k.at[j, 4], (to, h))

    def sib_forward(j, slot, n):
        return rcopy(
            kv.at[slot, :, :, hs(j)], kv.at[slot + 1, :, :, hs(j)], s_k.at[j, 4 + n], r_k.at[j, slot + 1], (sib, h)
        )

    for i in range(1, N_HEAD):
        q_copy(i).start()
    for n in range(3):
        k_copy(0, n).start()
    for i in range(1, N_HEAD):
        t_copy(i).start()
    for i in range(N_HEAD):
        p_copy(i).start()
    for one in wloads:
        one.start()

    mx[...] = jnp.full_like(mx, -1e30)
    acc[...] = jnp.zeros_like(acc)

    def wait_block(dst, sem):
        rcopy(dst, dst, sem, sem, (p, h)).wait_recv()

    def rows_of(source):
        return pl.ds(64 * source, 64)

    loads[0].wait()
    for i in range(1, N_HEAD):
        source = peer(i)
        wait_block(q_buf.at[pl.ds(pl.multiple_of(64 * source, 64), 64), :], r_q.at[source])
    loads[1].wait()
    for i in range(1, N_HEAD):
        source = peer(i)
        wait_block(tq.at[source], r_t.at[source])
    mine_text = tq[pl.ds(4 * x, 4)].astype(jnp.float32).reshape(32, W3).astype(jnp.bfloat16)
    q_buf[GR:MINE, :] = mine_text
    other_text = tq[pl.ds(4 - 4 * x, 4)].astype(jnp.float32).reshape(32, W3).astype(jnp.bfloat16)
    q_buf[MINE + GR : ROWS, :] = other_text
    for i in range(N_HEAD):
        source = peer(i)
        wait_block(q_buf.at[pl.ds(pl.multiple_of(MINE + 64 * source, 32), 64), :], r_p.at[source])
    loads[2].wait()

    for i in range(1, N_HEAD):
        for n in range(2):
            f_copy(i, n).start()

    @pl.when(text_here)
    def _():
        for i in range(1, N_HEAD):
            for n in range(2):
                x_copy(i, n).start()

    def attend(j, first, count, keys, values):
        rows = slice(first, first + count)
        scores = lax.dot_general(
            q_buf[rows, hs(j)], keys, (((1,), (1,)), ((), ())), preferred_element_type=jnp.float32
        )
        old = mx[j, rows, :]
        new = jnp.maximum(old, jnp.max(scores, axis=1, keepdims=True) * LOG2E_SCALE)
        weights = jnp.exp2(scores * LOG2E_SCALE - new[:, :1]).astype(jnp.bfloat16)
        decay = jnp.exp2(old - new)
        mx[j, rows, :] = new
        wide = jnp.concatenate([values, jnp.ones_like(values)], axis=1)
        mixed = jnp.dot(weights, wide, preferred_element_type=jnp.float32)
        acc[j, rows, :HD] = acc[j, rows, :HD] * decay + mixed[:, :HD]
        acc[j, rows, HD:] = acc[j, rows, HD:] * decay + mixed[:, HD:]

    def finish_partner(j):
        rows = slice(MINE, ROWS)
        sums = acc[j, rows, HD:]
        po[j] = (acc[j, rows, :HD] / sums).astype(jnp.bfloat16)
        lse = mx[j, rows, :] + jnp.log2(sums)
        lse = jnp.concatenate([lse, jnp.zeros((640 - MINE, HD), jnp.float32)], axis=0)
        ls[j] = jnp.transpose(lse)[:8, :]

    def o_copy(j, n):
        if n == 0:
            return rcopy(po.at[j], pr.at[j], s_o.at[j, 0], r_o.at[j, 0], (part, h))
        return rcopy(ls.at[j], lr.at[j], s_o.at[j, 1], r_o.at[j, 1], (part, h))

    def b_copy(j, i):
        to = peer(i)
        return rcopy(
            fin.at[j, pl.ds(pl.multiple_of(64 * to, 64), 64), :],
            attn.at[j, :, pl.ds(pl.multiple_of(h * HD, HD), HD)],
            s_b.at[j, i], r_b.at[j, h], (p, to),
        )

    def b_local(j):
        return pltpu.make_async_copy(
            fin.at[j, own_rows, :], attn.at[j, :, pl.ds(pl.multiple_of(h * HD, HD), HD)], lsem.at[9 + j]
        )

    def combine(j):
        wait_block(pr.at[j], r_o.at[j, 0])
        wait_block(lr.at[j], r_o.at[j, 1])
        row = lr[j]
        theirs = jnp.transpose(jnp.concatenate([row] * 16, axis=0))[:MINE, :]
        mine = mx[j, :MINE, :]
        top = jnp.maximum(mine, theirs)
        a = jnp.exp2(mine - top)
        b = jnp.exp2(theirs - top)
        both = acc[j, :MINE, :HD] * a + pr[j].astype(jnp.float32) * b
        done = both / (acc[j, :MINE, HD:] * a + b)
        fin[j] = done[:GR].astype(jnp.bfloat16)
        tfin[:, :, j * HD : (j + 1) * HD] = done[GR:].reshape(4, 8, HD).astype(jnp.bfloat16)
        for i in range(1, N_HEAD):
            b_copy(j, i).start()
        b_local(j).start()

    def project(j):
        b_local(j).wait()
        for i in range(1, N_HEAD):
            source = peer(i)
            wait_block(attn.at[j, :, pl.ds(pl.multiple_of(source * HD, HD), HD)], r_b.at[j, source])
        for g in range(N_HEAD):
            wloads[j * N_HEAD + g].wait()
        rows = attn[j]

        def tile(n, _):
            part_cols = pl.ds(pl.multiple_of(n * 512, 512), 512)
            prod = jnp.dot(rows, wbuf[j, :, part_cols], preferred_element_type=jnp.float32)
            if j == 0:
                total[:, part_cols] = prod
            else:
                total[:, part_cols] = total[:, part_cols] + prod
            return 0

        lax.fori_loop(0, D // 512, tile, 0)

    for j in range(NH):
        attend(j, GR, ROWS - GR, kv[0, 0, :, hs(j)], kv[0, 1, :, hs(j)])

        def block(i, _, j=j):
            slot = pick(i, SLOTS)
            wait_block(kv.at[slot, :, :, hs(j)], r_k.at[j, slot])

            @pl.when(i == 1)
            def _():
                sib_forward(j, 2, 0).start()

                @pl.when(c == 0)
                def _():
                    z_forward(j).start()

                if j + 1 < NH:
                    k_copy(j + 1, 1).start()

            @pl.when(i == 2)
            def _():
                sib_forward(j, 6, 1).start()

                @pl.when(c == 1)
                def _():
                    z_forward(j).start()

                if j + 1 < NH:
                    k_copy(j + 1, 2).start()
                    k_copy(j + 1, 0).start()

            @pl.when(i == 5)
            def _():
                sib_forward(j, 4, 2).start()

            keys, values = kv[slot, 0, :, hs(j)], kv[slot, 1, :, hs(j)]
            attend(j, 0, MINE, keys, values)
            attend(j, MINE, MINE, keys, values)
            return 0

        lax.fori_loop(0, len(SLOTS), block, 0)
        if j == 0:
            for n in range(2):
                loads[3 + n].wait()
            for i in range(1, N_HEAD):
                source = peer(i)
                for n in range(2):
                    wait_block(fresh.at[n, pl.ds(pl.multiple_of(64 * source, 64), 64), :], r_f.at[n, source])
            for g in range(4):
                for n in range(2):

                    @pl.when(h == 4 * x + g)
                    def _():
                        tlocal[n].wait()

                    @pl.when(h != 4 * x + g)
                    def _():
                        wait_block(tkv.at[n, pl.ds(64 * g, 64), :], r_x.at[n, g])

        attend(j, 0, GR, fresh[0, :, hs(j)], fresh[1, :, hs(j)])
        keys, values = tkv[0, :, hs(j)], tkv[1, :, hs(j)]
        attend(j, 0, MINE, keys, values)
        attend(j, MINE, MINE, keys, values)
        finish_partner(j)
        for n in range(2):
            o_copy(j, n).start()
        if j >= 1:
            combine(j - 1)

    project(0)
    combine(2)

    def ta_copy(g):
        to = 4 * x + g
        return rcopy(
            tfin.at[g], tattn.at[:, cols(0, h)], s_ta.at[g], r_ta.at[h], (p, to)
        )

    def ta_local(g):
        return pltpu.make_async_copy(tfin.at[g], tattn.at[:, cols(0, h)], lsem.at[12])

    for g in range(4):

        @pl.when(h == 4 * x + g)
        def _():
            ta_local(g).start()

        @pl.when(h != 4 * x + g)
        def _():
            ta_copy(g).start()

    project(1)

    def tb_copy(i):
        other = (p + i) % 16
        return rcopy(tattn, out_txt.at[t], s_tb.at[i], r_tb.at[t], (other, h))

    tb_local = pltpu.make_async_copy(tattn, out_txt.at[t], lsem.at[13])

    @pl.when(text_here)
    def _():
        ta_local(0).wait()
        for i in range(1, N_HEAD):
            source = peer(i)
            wait_block(tattn.at[:, cols(0, source)], r_ta.at[source])
        for i in range(1, 16):
            tb_copy(i).start()
        tb_local.start()

    project(2)
    loads[5].wait()
    loads[6].wait()
    obuf[...] = (res[...].astype(jnp.float32) + gat[...] * total[...]).astype(jnp.bfloat16)
    out_copy = pltpu.make_async_copy(obuf, out_img, lsem.at[14])
    out_copy.start()

    for n in range(8):

        @pl.when(jnp.logical_and(text_here, t == n))
        def _():
            tb_local.wait()

        @pl.when(jnp.logical_not(jnp.logical_and(text_here, t == n)))
        def _():
            wait_block(out_txt.at[n], r_tb.at[n])

    for i in range(1, N_HEAD):
        q_copy(i).wait_send()
        t_copy(i).wait_send()
        for n in range(2):
            f_copy(i, n).wait_send()
        for j in range(NH):
            b_copy(j, i).wait_send()
    for i in range(N_HEAD):
        p_copy(i).wait_send()

    @pl.when(text_here)
    def _():
        for i in range(1, N_HEAD):
            for n in range(2):
                x_copy(i, n).wait_send()
        for i in range(1, 16):
            tb_copy(i).wait_send()

    for g in range(4):

        @pl.when(h != 4 * x + g)
        def _():
            ta_copy(g).wait_send()

    for j in range(NH):
        for n in range(3):
            k_copy(j, n).wait_send()
        z_forward(j).wait_send()
        for n, slot in enumerate((2, 6, 4)):
            sib_forward(j, slot, n).wait_send()
        for n in range(2):
            o_copy(j, n).wait_send()
    out_copy.wait()


def per_device(img_qkv, txt_qkv, stale_kv, residual, gate_scale, proj_weight):
    any_space = pl.BlockSpec(memory_space=pl.ANY)
    bf, f32 = jnp.bfloat16, jnp.float32
    dma = pltpu.SemaphoreType.DMA
    image_out, text_out = pl.pallas_call(
        kernel,
        out_shape=(jax.ShapeDtypeStruct((64, D), bf), jax.ShapeDtypeStruct((8, 8, D), bf)),
        in_specs=[any_space] * 6,
        out_specs=(any_space, any_space),
        scratch_shapes=[
            pltpu.VMEM((ROWS, W3), bf),
            pltpu.VMEM((8, 8, W3), bf),
            pltpu.VMEM((8, 2, GR, W3), bf),
            pltpu.VMEM((2, GR, W3), bf),
            pltpu.VMEM((2, 256, W3), bf),
            pltpu.VMEM((NH, ROWS, 2 * HD), f32),
            pltpu.VMEM((NH, ROWS, HD), f32),
            pltpu.VMEM((NH, N_HEAD * HD, D), bf),
            pltpu.VMEM((NH, MINE, HD), bf),
            pltpu.VMEM((NH, MINE, HD), bf),
            pltpu.VMEM((NH, 8, 640), f32),
            pltpu.VMEM((NH, 8, 640), f32),
            pltpu.VMEM((NH, GR, HD), bf),
            pltpu.VMEM((4, 8, W3), bf),
            pltpu.VMEM((8, D), bf),
            pltpu.VMEM((NH, 64, N_HEAD * HD), bf),
            pltpu.VMEM((64, D), f32),
            pltpu.VMEM((64, D), bf),
            pltpu.VMEM((1, D), f32),
            pltpu.VMEM((64, D), bf),
            dma((8,)), dma((8,)),
            dma((8,)), dma((8,)),
            dma((8,)), dma((8,)),
            dma((2, 8)), dma((2, 8)),
            dma((2, 8)), dma((2, 4)),
            dma((NH, 7)), dma((NH, 8)),
            dma((NH, 2)), dma((NH, 2)),
            dma((NH, 8)), dma((NH, 8)),
            dma((4,)), dma((8,)),
            dma((16,)), dma((8,)),
            dma((15,)), dma((24,)),
        ],
        compiler_params=pltpu.CompilerParams(
            collective_id=0, has_side_effects=True, vmem_limit_bytes=62 * 1024 * 1024
        ),
    )(img_qkv, txt_qkv, stale_kv, residual, gate_scale.reshape(1, D), proj_weight)
    return image_out, text_out.reshape(64, D)


def solution(mesh):
    return jax.shard_map(
        per_device,
        mesh=mesh,
        in_specs=(
            P(("patch", "head"), None),
            P("head", None),
            P(None, "patch", "head"),
            P(("patch", "head"), None),
            P(),
            P(),
        ),
        out_specs=(P(("patch", "head"), None), P("head", None)),
        check_vma=False,
    )
```
